32 devices in a mesh: batch: 4 (over z), neg: 2 (over y), weight: 4 (over x, core).
Axes of the slice: x: 2, y: 2, z: 4, core: 2. Of those that a mesh axis runs over, the one named last changes fastest.
Arguments:
- images: bfloat16 [1024, 2048], P('batch'), may hold values from -30 to 30
- img_pair: int32 [1024], P('batch'), may hold values from 0 to 1023, each once
- texts: bfloat16 [1024, 2048], P(('batch', 'neg', 'weight')), may hold values from -100 to 100
- txt_pair: int32 [1024], P(('batch', 'neg', 'weight')), may hold values from 0 to 1023, each once
- gain: float32 [2048], replicated, may hold values from 0.1 to 1.9
- perm: int32 [2048], replicated, may hold values from 0 to 2047, each once
- right_blocks: bfloat16 [32, 64, 64], P('weight'), may hold values from -0.75 to 0.75
- left_blocks: bfloat16 [32, 64, 64], P('weight'), may hold values from -0.75 to 0.75
Outputs:
- grad_img: bfloat16 [1024, 2048], P(('batch', 'neg', 'weight'))
- row_loss: float32 [1024], P('batch')
The draws below stay inside these ranges and needn't reach their ends.
Inputs may be any that keep to these rules, and one draw needn't show every extreme that they name: Every pair id appears once in img_pair and once in txt_pair.
All inputs are finite; a program needn't handle non-finite values.
Results may differ from the reference program's by a relative error of at most 0.0065.
Values may be sent and summed in bfloat16 or wider, within the bound.
A program may use at most 64 MiB of HBM per device.

```python
import math
import jax
import jax.numpy as jnp
from jax import lax

D = 2048
BS = 64
NB = 32
BATCH = 1024


def image_base(key):
    folded = jax.random.fold_in(key, 101)
    normal_key = jax.random.fold_in(folded, 0)
    values = jnp.clip(jax.random.normal(normal_key, (BATCH, D), jnp.float32), -6.0, 6.0)
    return values


def draw_images(key, part):
    values = image_base(key)
    return values.astype(jnp.bfloat16)


def draw_texts(key, part):
    own_key = jax.random.fold_in(key, 202)
    base_key = jax.random.fold_in(own_key, 0)
    return jnp.clip(jax.random.normal(base_key, (BATCH, D), jnp.float32), -6.0, 6.0).astype(jnp.bfloat16)


def level_of(key, dims, shards, low, largest):
    def one(position, shards_of):
        heights = jax.random.uniform(jax.random.fold_in(jax.random.fold_in(key, 6), position), (shards_of,), jnp.float32, low / len(shards), largest / len(shards))
        return jnp.repeat(jnp.exp(heights), dims[position] // shards_of).reshape((-1,) + (1,) * (len(dims) - position - 1))

    loudness = one(*shards[0])
    for cut in shards[1:]:
        loudness = loudness * one(*cut)
    return loudness


def gaussian(stream_key, shape, width, bound, cuts=(), dtype=jnp.bfloat16):
    result = width * jax.random.normal(stream_key, shape, jnp.float32)
    if cuts:
        result = result * level_of(stream_key, shape, cuts, -0.22, 0.18)
    return jnp.clip(result, -bound, bound).astype(dtype)


def setup_inputs(seed: int = 0) -> dict:
    key_list = jax.random.split(jax.random.key(seed), 9)
    images = draw_images(jax.random.fold_in(key_list[8], 71), 0)
    img_pair = jax.random.permutation(key_list[1], BATCH).astype(jnp.int32)
    texts = draw_texts(jax.random.fold_in(key_list[8], 71), 0)
    txt_pair = jax.random.permutation(key_list[3], BATCH).astype(jnp.int32)
    gain = jnp.clip(1.0 + 0.18 * jax.random.normal(key_list[4], (D,), jnp.float32), 0.1, 1.9)
    perm = jax.random.permutation(key_list[5], D).astype(jnp.int32)
    right_blocks = gaussian(key_list[6], (NB, BS, BS), BS ** -0.5, 0.75, ((0, 4),))
    left_blocks = gaussian(key_list[7], (NB, BS, BS), BS ** -0.5, 0.75, ((0, 4),))
    return dict(images=images, img_pair=img_pair, texts=texts, txt_pair=txt_pair, gain=gain, perm=perm, right_blocks=right_blocks, left_blocks=left_blocks)


LOGIT_GAIN = 2.8

def monarch(images, gain, perm, right_blocks, left_blocks):
    values = images.astype(jnp.float32)
    row_count = values.shape[0]
    row_mean = lax.optimization_barrier(jnp.mean(values, axis=1, keepdims=True))
    centered = values - row_mean
    row_var = lax.optimization_barrier(jnp.mean(centered * centered, axis=1, keepdims=True))
    normed = (centered * lax.rsqrt(row_var + 1e-05) * gain).astype(jnp.bfloat16)
    inner_mixed = jnp.einsum('rke,kec->rkc', normed.reshape(row_count, NB, BS).astype(jnp.float32), right_blocks.astype(jnp.float32))
    active = jax.nn.gelu(inner_mixed, approximate=True).astype(jnp.bfloat16).reshape(row_count, D)
    permuted = jnp.take(active, perm, axis=1)
    outer_mixed = jnp.einsum('rke,kec->rkc', permuted.reshape(row_count, NB, BS).astype(jnp.float32), left_blocks.astype(jnp.float32))
    return (values + outer_mixed.reshape(row_count, D)).astype(jnp.bfloat16)

def reference(images, img_pair, texts, txt_pair, gain, perm, right_blocks, left_blocks):
    logit_scale = LOGIT_GAIN / math.sqrt(D)
    blocks = 16
    row_count = BATCH // blocks

    def per_block(block_pair):
        image_rows, pair_rows = block_pair
        embedded = monarch(image_rows, gain, perm, right_blocks, left_blocks)
        scores = jnp.dot(embedded, texts.T, preferred_element_type=jnp.float32) * logit_scale
        matches = (pair_rows[:, None] == txt_pair[None, :]).astype(jnp.float32)
        row_max = lax.optimization_barrier(jnp.max(scores, axis=1))
        shifted = jnp.exp(scores - row_max[:, None])
        totals = lax.optimization_barrier(jnp.sum(shifted, axis=1))
        positive = lax.optimization_barrier(jnp.sum(matches * scores, axis=1))
        row_loss = row_max + jnp.log(totals) - positive
        dscore = (shifted / totals[:, None] - matches).astype(jnp.bfloat16)
        grads = jnp.dot(dscore, texts, preferred_element_type=jnp.float32).astype(jnp.bfloat16)
        return (grads, row_loss)
    grads, losses = lax.map(per_block, (images.reshape(blocks, row_count, D), img_pair.reshape(blocks, row_count)))
    return (grads.reshape(BATCH, D), losses.reshape(BATCH))
```

```python
import functools
import math

import jax
import jax.numpy as jnp
from jax import lax
from jax.experimental import pallas as pl
from jax.experimental.pallas import tpu as pltpu
from jax.sharding import PartitionSpec as P

LOGIT_GAIN = 2.8
MESH = pl.DeviceIdType.MESH
F32, BF16 = jnp.float32, jnp.bfloat16
VMEM_FOR_TEXTS = 16 * 2**20


def plane_orders(count):
    return [sorted(range(count), key=lambda o: (abs(o - own), o)) for own in range(count)]


def block_diagonal(wide):
    size = wide.shape[0]
    lane = lax.broadcasted_iota(jnp.int32, wide.shape, 1)
    values = wide.astype(F32)
    upper = jnp.where(lane < size, values, 0.0)
    lower = jnp.where(lane < size, 0.0, values)
    return jnp.concatenate([upper, lower], axis=0).astype(BF16)


def fused_kernel(
    dims, images_ref, img_pair_ref, texts_ref, txt_pair_ref, gain_ref, perm_ref, right_ref, left_ref,
    grad_ref, loss_ref,
    rows_ref, wts, buf, pairs, normed_ref, active_ref, permuted_ref, emb_ref, score_ref, losses,
    local_sem, wt_send, wt_recv, send_sem, recv_sem, pair_send, pair_recv, loss_send, loss_recv,
):
    nb, nn, nw = dims
    width = texts_ref.shape[1]
    t_rows = texts_ref.shape[0]
    block_count, size = right_ref.shape[0], right_ref.shape[1]
    pair_count = block_count // 2
    lanes = 2 * size
    r_rows = rows_ref.shape[0]
    group = nn * nw
    b, n, w = lax.axis_index("batch"), lax.axis_index("neg"), lax.axis_index("weight")
    core = lax.rem(w, 2)
    far = 1 - 2 * lax.div(w, 2)
    flip = 1 - 2 * n
    n_a, w_a = n + core * flip, w + (1 - core) * 2 * far
    n_b, w_b = n + (1 - core) * flip, w + core * 2 * far
    n_d, w_d = 1 - n, w + 2 * far
    w_p = w + 1 - 2 * core
    dev_a, dev_b, dev_p = (b, n_a, w_a), (b, n_b, w_b), (b, n, w_p)
    dev_x = (b, n, w_d)
    dev_up, dev_down = (b + 1, n, w), (b - 1, n, w)
    me = n * nw + w

    def slot(o, nn_, ww_):
        return (o * nn + nn_) * nw + ww_

    orders = plane_orders(nb)

    def origin(k):
        value = jnp.int32(orders[0][k])
        for own in range(1, nb):
            value = jnp.where(b == own, orders[own][k], value)
        return value

    planes = [origin(k) for k in range(nb)]

    own_slot = slot(b, n, w)
    copy_rows = pltpu.make_async_copy(images_ref.at[pl.ds(pl.multiple_of(me * r_rows, r_rows), r_rows)], rows_ref, local_sem.at[0])
    copy_text = pltpu.make_async_copy(texts_ref, buf.at[own_slot], local_sem.at[1])
    copy_rows.start()
    copy_text.start()
    for k in range(pair_count):
        wts[w, k] = jnp.concatenate([right_ref[2 * k], right_ref[2 * k + 1]], axis=1)
        wts[w, pair_count + k] = jnp.concatenate([left_ref[2 * k], left_ref[2 * k + 1]], axis=1)
    ids = txt_pair_ref[...]
    pairs[own_slot] = jnp.concatenate([ids] * nw, axis=1)

    barrier = pltpu.get_barrier_semaphore()
    near = [dev_a, dev_b, dev_p, (b, n_d, w_d)]
    near += [(b, n_a, w_a + 1 - 2 * core), (b, n_b, w_b + 1 - 2 * core), (b, n_d, w_d + 1 - 2 * core)]
    for dev in near:
        pl.semaphore_signal(barrier, inc=1, device_id=dev, device_id_type=MESH)

    @pl.when(b < nb - 1)
    def _():
        pl.semaphore_signal(barrier, inc=1, device_id=dev_up, device_id_type=MESH)

    @pl.when(b > 0)
    def _():
        pl.semaphore_signal(barrier, inc=1, device_id=dev_down, device_id_type=MESH)

    expected = len(near) + jnp.where(b < nb - 1, 1, 0) + jnp.where(b > 0, 1, 0)
    pl.semaphore_wait(barrier, expected)

    def weight_copy(index, kind, dev):
        return pltpu.make_async_remote_copy(
            src_ref=wts.at[index], dst_ref=wts.at[index], send_sem=wt_send.at[kind], recv_sem=wt_recv.at[index],
            device_id=dev, device_id_type=MESH,
        )

    weight_copy(w, 0, dev_x).start()
    weight_copy(w, 1, dev_p).start()

    def text_copy(index, kind, dev, source):
        return pltpu.make_async_remote_copy(
            src_ref=source, dst_ref=buf.at[index], send_sem=send_sem.at[index, kind], recv_sem=recv_sem.at[index],
            device_id=dev, device_id_type=MESH,
        )

    def pair_copy(index, kind, dev):
        return pltpu.make_async_remote_copy(
            src_ref=pairs.at[index], dst_ref=pairs.at[index], send_sem=pair_send.at[index, kind],
            recv_sem=pair_recv.at[index], device_id=dev, device_id_type=MESH,
        )

    sent = []

    def send(index, kind, dev, source=None, when=None):
        text = text_copy(index, kind, dev, buf.at[index] if source is None else source)
        pair = pair_copy(index, kind, dev)

        def begin():
            text.start()
            pair.start()

        def finish():
            text.wait_send()
            pair.wait_send()

        if when is None:
            begin()
            sent.append(finish)
        else:
            pl.when(when)(begin)
            sent.append(lambda: pl.when(when)(finish))

    def arrive(index):
        text_copy(index, 0, dev_a, buf.at[index]).wait_recv()
        pair_copy(index, 0, dev_a).wait_recv()

    def column(k):
        o = planes[k]
        index = slot(o, n, w)
        if k > 0:
            arrive(index)
        source = texts_ref if k == 0 else None
        send(index, 3, dev_up, source, (o <= b) & (b < nb - 1))
        send(index, 4, dev_down, source, (o >= b) & (b > 0))
        send(index, 0, dev_a, source)
        send(index, 1, dev_b, source)
        send(index, 2, dev_p, source)

    def from_a(k):
        index = slot(planes[k], n_a, w_a)
        arrive(index)
        send(index, 1, dev_b)
        send(index, 2, dev_p)

    def from_b(k):
        index = slot(planes[k], n_b, w_b)
        arrive(index)
        send(index, 2, dev_p)

    def diagonal(k):
        index = slot(planes[k], n_d, w_d)
        arrive(index)
        send(index, 2, dev_p)

    def from_partner(k):
        for nn_ in range(nn):
            for half in range(nw // 2):
                arrive(slot(planes[k], nn_, 2 * half + 1 - core))

    column(0)

    copy_rows.wait()
    values = rows_ref[...].astype(F32)
    mean = jnp.sum(values, axis=1, keepdims=True) / width
    centered = values - mean
    var = jnp.sum(centered * centered, axis=1, keepdims=True) / width
    normed_ref[...] = (centered * lax.rsqrt(var + 1e-05) * gain_ref[...]).astype(BF16)

    column(1)
    from_a(0)
    from_b(0)

    weight_copy(w_d, 0, dev_x).wait_recv()
    weight_copy(w_d, 2, dev_p).start()
    weight_copy(w_p, 0, dev_x).wait_recv()
    weight_copy(w_d + 1 - 2 * core, 0, dev_x).wait_recv()

    for s in range(nw):
        for k in range(pair_count):
            at = (s * pair_count + k) * lanes
            inner = jnp.dot(
                normed_ref[:, at : at + lanes], block_diagonal(wts[s, k]), preferred_element_type=F32
            )
            active_ref[:, at : at + lanes] = jax.nn.gelu(inner, approximate=True).astype(BF16)

    column(2)
    from_a(1)
    from_b(1)

    step = 2 * lanes
    row_id = lax.broadcasted_iota(jnp.int32, (width, step), 0)

    def permute(lo, hi):
        @pl.loop(lo, hi)
        def _(c):
            at = pl.ds(pl.multiple_of(c * step, step), step)
            chosen = jnp.where(row_id == perm_ref[:, at], 1.0, 0.0).astype(BF16)
            permuted_ref[:, at] = jnp.dot(active_ref[...], chosen, preferred_element_type=F32).astype(BF16)

    chunks = width // step
    permute(0, chunks // 4)
    diagonal(0)
    for k in range(3, nb):
        column(k)
    permute(chunks // 4, chunks // 2)
    from_a(2)
    from_b(2)
    permute(chunks // 2, chunks)
    diagonal(1)

    for s in range(nw):
        for k in range(pair_count):
            at = (s * pair_count + k) * lanes
            outer = jnp.dot(
                permuted_ref[:, at : at + lanes], block_diagonal(wts[s, pair_count + k]), preferred_element_type=F32
            )
            emb_ref[:, at : at + lanes] = (rows_ref[:, at : at + lanes].astype(F32) + outer).astype(BF16)

    logit_scale = LOGIT_GAIN / math.sqrt(width)
    copy_text.wait()

    def scores(k):
        from_partner(k)
        block = buf[pl.ds(planes[k] * group, group)].reshape(group * t_rows, width)
        product = lax.dot_general(emb_ref[...], block, (((1,), (1,)), ((), ())), preferred_element_type=F32)
        score_ref[planes[k]] = product * logit_scale

    for k in range(3, nb):
        from_a(k)
        from_b(k)
    scores(0)
    diagonal(2)
    scores(1)
    for k in range(3, nb):
        diagonal(k)
    for k in range(2, nb):
        scores(k)

    columns = group * t_rows
    total_rows = img_pair_ref.shape[1]
    place = lax.broadcasted_iota(jnp.int32, (r_rows, total_rows), 1) == (
        lax.broadcasted_iota(jnp.int32, (r_rows, total_rows), 0) + me * r_rows
    )
    own_ids = jnp.sum(jnp.where(place, img_pair_ref[...], 0), axis=1, keepdims=True)
    quarter = lax.broadcasted_iota(jnp.int32, (1, nw * t_rows), 1) // t_rows

    def pair_row(first):
        row = pairs[first]
        for ww_ in range(1, nw):
            row = jnp.where(quarter == ww_, pairs[first + ww_], row)
        return row

    found = [
        own_ids == jnp.concatenate([pair_row(slot(o, nn_, 0)) for nn_ in range(nn)], axis=1) for o in range(nb)
    ]
    parts = [score_ref[o] for o in range(nb)]
    row_max = functools.reduce(jnp.maximum, [jnp.max(part, axis=1, keepdims=True) for part in parts])
    shifted = [jnp.exp(part - row_max) for part in parts]
    totals = functools.reduce(jnp.add, [jnp.sum(part, axis=1, keepdims=True) for part in shifted])
    positive = functools.reduce(
        jnp.add, [jnp.sum(jnp.where(hit, part, 0.0), axis=1, keepdims=True) for hit, part in zip(found, parts)]
    )
    row_loss = row_max + jnp.log(totals) - positive
    losses[me] = jnp.sum(jnp.where(place, row_loss, 0.0), axis=0, keepdims=True)
    dscore = [
        (part / totals - jnp.where(hit, 1.0, 0.0)).astype(BF16) for hit, part in zip(found, shifted)
    ]

    tile = width // 4

    def gradient(c):
        at = slice(c * tile, (c + 1) * tile)
        total = jnp.zeros((r_rows, tile), F32)
        for o in range(nb):
            block = buf[o * group : (o + 1) * group, :, at].reshape(columns, tile)
            total = total + jnp.dot(dscore[o], block, preferred_element_type=F32)
        grad_ref[:, at] = total.astype(BF16)

    gradient(0)
    loss_copies = []
    for position, dev in enumerate(near):
        loss_copies.append(
            pltpu.make_async_remote_copy(
                src_ref=losses.at[me], dst_ref=losses.at[me], send_sem=loss_send.at[position],
                recv_sem=loss_recv.at[me], device_id=dev, device_id_type=MESH,
            )
        )
        loss_copies[-1].start()
    for c in range(1, 4):
        gradient(c)
    for _, n_o, w_o in near:
        other = n_o * nw + w_o
        pltpu.make_async_remote_copy(
            src_ref=losses.at[other], dst_ref=losses.at[other], send_sem=loss_send.at[0],
            recv_sem=loss_recv.at[other], device_id=dev_p, device_id_type=MESH,
        ).wait_recv()
    loss_ref[...] = functools.reduce(jnp.add, [losses[i] for i in range(group)])

    for finish in sent:
        finish()
    weight_copy(w, 0, dev_x).wait_send()
    weight_copy(w, 1, dev_p).wait_send()
    weight_copy(w_d, 2, dev_p).wait_send()
    for copy in loss_copies:
        copy.wait_send()


def fused(dims, images, img_pair, texts, txt_pair, gain, perm, right_blocks, left_blocks):
    nb, nn, nw = dims
    group = nn * nw
    devices = nb * group
    t_rows, width = texts.shape
    r_rows = images.shape[0] // group
    block_count, size = right_blocks.shape[:2]
    vmem = pl.BlockSpec(memory_space=pltpu.VMEM)
    hbm = pl.BlockSpec(memory_space=pl.ANY)
    dma = pltpu.SemaphoreType.DMA
    grad, loss = pl.pallas_call(
        functools.partial(fused_kernel, dims),
        out_shape=(
            jax.ShapeDtypeStruct((r_rows, width), BF16),
            jax.ShapeDtypeStruct((1, images.shape[0]), F32),
        ),
        in_specs=[hbm, vmem, hbm, vmem, vmem, vmem, vmem, vmem],
        out_specs=(vmem, vmem),
        scratch_shapes=[
            pltpu.VMEM((r_rows, width), BF16),
            pltpu.VMEM((nw, block_count, size, 2 * size), BF16),
            pltpu.VMEM((devices, t_rows, width), BF16),
            pltpu.VMEM((devices, 1, nw * t_rows), jnp.int32),
            pltpu.VMEM((r_rows, width), BF16),
            pltpu.VMEM((r_rows, width), BF16),
            pltpu.VMEM((r_rows, width), BF16),
            pltpu.VMEM((r_rows, width), BF16),
            pltpu.VMEM((nb, r_rows, group * t_rows), F32),
            pltpu.VMEM((group, 1, images.shape[0]), F32),
            dma((2,)),
            dma((3,)),
            dma((nw,)),
            dma((devices, 5)),
            dma((devices,)),
            dma((devices, 5)),
            dma((devices,)),
            dma((group - 1,)),
            dma((group,)),
        ],
        compiler_params=pltpu.CompilerParams(
            collective_id=0, has_side_effects=True, vmem_limit_bytes=48 * 2**20
        ),
    )(
        images, img_pair[None], texts, txt_pair[None], gain[None], perm[None], right_blocks, left_blocks
    )
    return grad, loss[0]


def monarch(images, gain, perm, right_full, left_full):
    row_count, width = images.shape
    block_count, block_size = (right_full.shape[0], right_full.shape[1])
    values = images.astype(jnp.float32)
    row_mean = jnp.mean(values, axis=1, keepdims=True)
    centered = values - row_mean
    row_var = jnp.mean(centered * centered, axis=1, keepdims=True)
    normed = (centered * lax.rsqrt(row_var + 1e-05) * gain).astype(jnp.bfloat16)
    inner_mixed = jnp.einsum(
        "rke,kec->rkc",
        normed.reshape(row_count, block_count, block_size),
        right_full,
        preferred_element_type=jnp.float32,
    )
    active = (
        jax.nn.gelu(inner_mixed, approximate=True).astype(jnp.bfloat16).reshape(row_count, width)
    )
    permuted = jnp.take(active, perm, axis=1)
    outer_mixed = jnp.einsum(
        "rke,kec->rkc",
        permuted.reshape(row_count, block_count, block_size),
        left_full,
        preferred_element_type=jnp.float32,
    )
    return (values + outer_mixed.reshape(row_count, width)).astype(jnp.bfloat16)


def per_device(images, img_pair, texts, txt_pair, gain, perm, right_blocks, left_blocks):
    right_full, left_full = (
        lax.all_gather(right_blocks, "weight", axis=0, tiled=True),
        lax.all_gather(left_blocks, "weight", axis=0, tiled=True),
    )
    embedded = monarch(images, gain, perm, right_full, left_full)
    gathered, gathered_pair = (
        lax.all_gather(texts, "batch", axis=0, tiled=True),
        lax.all_gather(txt_pair, "batch", axis=0, tiled=True),
    )
    logit_scale = LOGIT_GAIN / math.sqrt(images.shape[1])
    scores = (
        jnp.einsum("rd,cd->rc", embedded, gathered, preferred_element_type=jnp.float32)
        * logit_scale
    )
    matches = (img_pair[:, None] == gathered_pair[None, :]).astype(jnp.float32)
    local_max = jnp.max(scores, axis=1)
    local_pos = jnp.sum(matches * scores, axis=1)
    row_max = lax.pmax(local_max, ("neg", "weight"))
    shifted = jnp.exp(scores - row_max[:, None])
    totals, positive = lax.psum((jnp.sum(shifted, axis=1), local_pos), ("neg", "weight"))
    row_loss = row_max + jnp.log(totals) - positive
    dscore = (shifted / totals[:, None] - matches).astype(jnp.bfloat16)
    grad_sum = lax.psum_scatter(
        jnp.dot(dscore, gathered, preferred_element_type=jnp.float32),
        ("neg", "weight"),
        scatter_dimension=0,
        tiled=True,
    )
    grad_img = grad_sum.astype(jnp.bfloat16)
    return (grad_img, row_loss)


def solution(mesh):
    dims = tuple(mesh.shape[axis] for axis in ("batch", "neg", "weight"))

    def body(images, img_pair, texts, txt_pair, gain, perm, right_blocks, left_blocks):
        args = (images, img_pair, texts, txt_pair, gain, perm, right_blocks, left_blocks)
        text_bytes = math.prod(dims) * texts.size * texts.dtype.itemsize
        if dims[1:] == (2, 4) and dims[0] >= 3 and text_bytes <= VMEM_FOR_TEXTS:
            return fused(dims, *args)
        return per_device(*args)

    return jax.shard_map(
        body,
        mesh=mesh,
        in_specs=(
            P("batch", None),
            P("batch"),
            P(("batch", "neg", "weight"), None),
            P(("batch", "neg", "weight")),
            P(),
            P(),
            P("weight", None, None),
            P("weight", None, None),
        ),
        out_specs=(P(("batch", "neg", "weight"), None), P("batch")),
        check_vma=False,
    )
```

```python
import functools
import math

import jax
import jax.numpy as jnp
from jax import lax
from jax.experimental import pallas as pl
from jax.experimental.pallas import tpu as pltpu
from jax.sharding import PartitionSpec as P

LOGIT_GAIN = 2.8
MESH = pl.DeviceIdType.MESH
F32, BF16 = jnp.float32, jnp.bfloat16
PARTS = 1
VMEM_FOR_TEXTS = 16 * 2**20


def plane_orders(count):
    return [sorted(range(count), key=lambda o: (abs(o - own), o)) for own in range(count)]


def block_diagonal(wide):
    size = wide.shape[0]
    lane = lax.broadcasted_iota(jnp.int32, wide.shape, 1)
    values = wide.astype(F32)
    upper = jnp.where(lane < size, values, 0.0)
    lower = jnp.where(lane < size, 0.0, values)
    return jnp.concatenate([upper, lower], axis=0).astype(BF16)


def fused_kernel(
    dims, images_hbm, img_pair_hbm, texts_ref, txt_pair_hbm, gain_hbm, perm_hbm, right_hbm, left_hbm,
    grad_ref, loss_ref, img_pair_ref, txt_pair_ref, gain_ref, perm_ref, right_ref, left_ref,
    rows_ref, wts, buf, pairs, normed_ref, active_ref, permuted_ref, emb_ref, score_ref, losses,
    local_sem, wt_send, wt_recv, send_sem, recv_sem, pair_send, pair_recv, loss_send, loss_recv,
):
    nb, nn, nw = dims
    width = texts_ref.shape[1]
    t_rows = texts_ref.shape[0]
    block_count, size = right_ref.shape[0], right_ref.shape[1]
    pair_count = block_count // 2
    lanes = 2 * size
    r_rows = rows_ref.shape[0]
    group = nn * nw
    b, n, w = lax.axis_index("batch"), lax.axis_index("neg"), lax.axis_index("weight")
    core = lax.rem(w, 2)
    far = 1 - 2 * lax.div(w, 2)
    flip = 1 - 2 * n
    n_a, w_a = n + core * flip, w + (1 - core) * 2 * far
    n_b, w_b = n + (1 - core) * flip, w + core * 2 * far
    n_d, w_d = 1 - n, w + 2 * far
    w_p = w + 1 - 2 * core
    dev_a, dev_b, dev_p = (b, n_a, w_a), (b, n_b, w_b), (b, n, w_p)
    dev_x = (b, n, w_d)
    dev_up, dev_down = (b + 1, n, w), (b - 1, n, w)
    me = n * nw + w

    def slot(o, nn_, ww_):
        return (o * nn + nn_) * nw + ww_

    orders = plane_orders(nb)

    def origin(k):
        value = jnp.int32(orders[0][k])
        for own in range(1, nb):
            value = jnp.where(b == own, orders[own][k], value)
        return value

    planes = [origin(k) for k in range(nb)]

    barrier = pltpu.get_barrier_semaphore()
    near = [dev_a, dev_b, dev_p, (b, n_d, w_d)]
    near += [(b, n_a, w_a + 1 - 2 * core), (b, n_b, w_b + 1 - 2 * core), (b, n_d, w_d + 1 - 2 * core)]
    for dev in near:
        pl.semaphore_signal(barrier, inc=1, device_id=dev, device_id_type=MESH)

    @pl.when(b < nb - 1)
    def _():
        pl.semaphore_signal(barrier, inc=1, device_id=dev_up, device_id_type=MESH)

    @pl.when(b > 0)
    def _():
        pl.semaphore_signal(barrier, inc=1, device_id=dev_down, device_id_type=MESH)

    own_slot = slot(b, n, w)
    staged = [
        pltpu.make_async_copy(source, target, local_sem.at[2 + i])
        for i, (source, target) in enumerate([
            (right_hbm, right_ref), (left_hbm, left_ref), (txt_pair_hbm, txt_pair_ref),
            (gain_hbm, gain_ref), (perm_hbm, perm_ref), (img_pair_hbm, img_pair_ref),
        ])
    ]
    for copy in staged:
        copy.start()
    copy_rows = pltpu.make_async_copy(images_hbm.at[pl.ds(pl.multiple_of(me * r_rows, r_rows), r_rows)], rows_ref, local_sem.at[0])
    copy_text = pltpu.make_async_copy(texts_ref, buf.at[own_slot], local_sem.at[1])
    copy_rows.start()
    copy_text.start()
    expected = len(near) + jnp.where(b < nb - 1, 1, 0) + jnp.where(b > 0, 1, 0)
    pl.semaphore_wait(barrier, expected)

    def weight_copy(index, kind, dev):
        return pltpu.make_async_remote_copy(
            src_ref=wts.at[index], dst_ref=wts.at[index], send_sem=wt_send.at[kind], recv_sem=wt_recv.at[index],
            device_id=dev, device_id_type=MESH,
        )

    half = t_rows // PARTS

    def text_copy(index, kind, part, dev, source):
        rows = pl.ds(part * half, half)
        return pltpu.make_async_remote_copy(
            src_ref=source.at[rows], dst_ref=buf.at[index, rows], send_sem=send_sem.at[index, kind, part],
            recv_sem=recv_sem.at[index, part], device_id=dev, device_id_type=MESH,
        )

    def pair_copy(index, kind, dev):
        return pltpu.make_async_remote_copy(
            src_ref=pairs.at[index], dst_ref=pairs.at[index], send_sem=pair_send.at[index, kind],
            recv_sem=pair_recv.at[index], device_id=dev, device_id_type=MESH,
        )

    sent = []

    def launch(copy, when):
        if when is None:
            copy.start()
            sent.append(copy.wait_send)
        else:
            pl.when(when)(copy.start)
            sent.append(lambda: pl.when(when)(copy.wait_send))

    def send_text(index, kind, part, dev, source, when):
        launch(text_copy(index, kind, part, dev, source), when)

    def send_pair(index, kind, dev, when):
        launch(pair_copy(index, kind, dev), when)

    def send(index, kind, part, dev, when=None):
        send_text(index, kind, part, dev, buf.at[index], when)
        if part == PARTS - 1:
            send_pair(index, kind, dev, when)

    def arrive(index, part):
        text_copy(index, 0, part, dev_a, buf.at[index]).wait_recv()
        if part == PARTS - 1:
            pair_copy(index, 0, dev_a).wait_recv()

    def along_chain(o, receiver):
        distance = jnp.abs(o - receiver)
        return distance < 0

    def column(k):
        o = planes[k]
        index = slot(o, n, w)
        for part in range(PARTS):
            arrive(index, part)
            send(index, 3, part, dev_up, (o <= b) & (b < nb - 1))
            send(index, 4, part, dev_down, (o >= b) & (b > 0))
            send(index, 0, part, dev_a)
            send(index, 1, part, dev_b)
            send(index, 2, part, dev_p)

    def from_a(k):
        index = slot(planes[k], n_a, w_a)
        for part in range(PARTS):
            arrive(index, part)
            send(index, 1, part, dev_b, jnp.logical_not(along_chain(planes[k], b)) if k else None)
            send(index, 2, part, dev_p)

    def from_b(k):
        index = slot(planes[k], n_b, w_b)
        for part in range(PARTS):
            arrive(index, part)
            send(index, 2, part, dev_p)

    def diagonal(k):
        o = planes[k]
        index = slot(o, n_d, w_d)
        for part in range(PARTS):
            arrive(index, part)
            send(index, 3, part, dev_up, (o <= b) & (b < nb - 1) & along_chain(o, b + 1))
            send(index, 4, part, dev_down, (o >= b) & (b > 0) & along_chain(o, b - 1))
            send(index, 2, part, dev_p)

    def from_partner(k):
        for nn_ in range(nn):
            for ww_ in range(nw // 2):
                for part in range(PARTS):
                    arrive(slot(planes[k], nn_, 2 * ww_ + 1 - core), part)

    own_targets = [
        (3, dev_up, b < nb - 1), (4, dev_down, b > 0), (0, dev_a, None), (1, dev_b, None), (2, dev_p, None),
    ]

    def own_sends(part):
        for kind, dev, when in own_targets:
            send_text(own_slot, kind, part, dev, texts_ref, when)

    def layer_norm():
        copy_rows.wait()
        for copy in staged[3:]:
            copy.wait()
        values = rows_ref[...].astype(F32)
        mean = jnp.sum(values, axis=1, keepdims=True) / width
        centered = values - mean
        var = jnp.sum(centered * centered, axis=1, keepdims=True) / width
        normed_ref[...] = (centered * lax.rsqrt(var + 1e-05) * gain_ref[...]).astype(BF16)

    for part in range(PARTS):
        own_sends(part)

    for copy in staged[:3]:
        copy.wait()
    ids = txt_pair_ref[...]
    pairs[own_slot] = jnp.concatenate([ids] * nw, axis=1)
    for k in range(pair_count):
        wts[w, k] = jnp.concatenate([right_ref[2 * k], right_ref[2 * k + 1]], axis=1)
        wts[w, pair_count + k] = jnp.concatenate([left_ref[2 * k], left_ref[2 * k + 1]], axis=1)
    layer_norm()
    for kind, dev, when in own_targets:
        send_pair(own_slot, kind, dev, when)
    weight_copy(w, 0, dev_x).start()
    weight_copy(w, 1, dev_p).start()

    column(1)
    from_a(0)
    from_b(0)
    column(2)
    from_a(1)
    weight_copy(w_d, 0, dev_x).wait_recv()
    weight_copy(w_d, 2, dev_p).start()
    for k in range(3, nb):
        column(k)
    diagonal(0)
    from_b(1)
    from_a(2)
    weight_copy(w_p, 0, dev_x).wait_recv()
    weight_copy(w_d + 1 - 2 * core, 0, dev_x).wait_recv()
    diagonal(1)
    from_b(2)

    for s in range(nw):
        for k in range(pair_count):
            at = (s * pair_count + k) * lanes
            inner = jnp.dot(
                normed_ref[:, at : at + lanes], block_diagonal(wts[s, k]), preferred_element_type=F32
            )
            active_ref[:, at : at + lanes] = jax.nn.gelu(inner, approximate=True).astype(BF16)

    step = 2 * lanes
    row_id = lax.broadcasted_iota(jnp.int32, (width, step), 0)

    def permute(lo, hi):
        @pl.loop(lo, hi)
        def _(c):
            at = pl.ds(pl.multiple_of(c * step, step), step)
            chosen = jnp.where(row_id == perm_ref[:, at], 1.0, 0.0).astype(BF16)
            permuted_ref[:, at] = jnp.dot(active_ref[...], chosen, preferred_element_type=F32).astype(BF16)

    chunks = width // step
    for k in range(3, nb):
        from_a(k)
    permute(0, chunks // 2)
    for k in range(3, nb):
        from_b(k)
    permute(chunks // 2, chunks)

    for s in range(nw):
        for k in range(pair_count):
            at = (s * pair_count + k) * lanes
            outer = jnp.dot(
                permuted_ref[:, at : at + lanes], block_diagonal(wts[s, pair_count + k]), preferred_element_type=F32
            )
            emb_ref[:, at : at + lanes] = (rows_ref[:, at : at + lanes].astype(F32) + outer).astype(BF16)

    logit_scale = LOGIT_GAIN / math.sqrt(width)
    copy_text.wait()

    def scores(k):
        from_partner(k)
        block = buf[pl.ds(planes[k] * group, group)].reshape(group * t_rows, width)
        product = lax.dot_general(emb_ref[...], block, (((1,), (1,)), ((), ())), preferred_element_type=F32)
        score_ref[planes[k]] = product * logit_scale

    scores(0)
    diagonal(2)
    scores(1)
    for k in range(3, nb):
        diagonal(k)
    for k in range(2, nb):
        scores(k)

    columns = group * t_rows
    total_rows = img_pair_ref.shape[1]
    place = lax.broadcasted_iota(jnp.int32, (r_rows, total_rows), 1) == (
        lax.broadcasted_iota(jnp.int32, (r_rows, total_rows), 0) + me * r_rows
    )
    own_ids = jnp.sum(jnp.where(place, img_pair_ref[...], 0), axis=1, keepdims=True)
    quarter = lax.broadcasted_iota(jnp.int32, (1, nw * t_rows), 1) // t_rows

    def pair_row(first):
        row = pairs[first]
        for ww_ in range(1, nw):
            row = jnp.where(quarter == ww_, pairs[first + ww_], row)
        return row

    found = [
        own_ids == jnp.concatenate([pair_row(slot(o, nn_, 0)) for nn_ in range(nn)], axis=1) for o in range(nb)
    ]
    parts = [score_ref[o] for o in range(nb)]
    row_max = functools.reduce(jnp.maximum, [jnp.max(part, axis=1, keepdims=True) for part in parts])
    shifted = [jnp.exp(part - row_max) for part in parts]
    totals = functools.reduce(jnp.add, [jnp.sum(part, axis=1, keepdims=True) for part in shifted])
    positive = functools.reduce(
        jnp.add, [jnp.sum(jnp.where(hit, part, 0.0), axis=1, keepdims=True) for hit, part in zip(found, parts)]
    )
    row_loss = row_max + jnp.log(totals) - positive
    losses[me] = jnp.sum(jnp.where(place, row_loss, 0.0), axis=0, keepdims=True)
    dscore = [
        (part / totals - jnp.where(hit, 1.0, 0.0)).astype(BF16) for hit, part in zip(found, shifted)
    ]

    tile = width // 8

    def gradient(c):
        at = slice(c * tile, (c + 1) * tile)
        total = jnp.zeros((r_rows, tile), F32)
        for o in range(nb):
            block = buf[o * group : (o + 1) * group, :, at].reshape(columns, tile)
            total = total + jnp.dot(dscore[o], block, preferred_element_type=F32)
        grad_ref[:, at] = total.astype(BF16)

    gradient(0)
    loss_copies = []
    for position, dev in enumerate(near):
        loss_copies.append(
            pltpu.make_async_remote_copy(
                src_ref=losses.at[me], dst_ref=losses.at[me], send_sem=loss_send.at[position],
                recv_sem=loss_recv.at[me], device_id=dev, device_id_type=MESH,
            )
        )
        loss_copies[-1].start()
    for c in range(1, 8):
        gradient(c)
    for _, n_o, w_o in near:
        other = n_o * nw + w_o
        pltpu.make_async_remote_copy(
            src_ref=losses.at[other], dst_ref=losses.at[other], send_sem=loss_send.at[0],
            recv_sem=loss_recv.at[other], device_id=dev_p, device_id_type=MESH,
        ).wait_recv()
    loss_ref[...] = functools.reduce(jnp.add, [losses[i] for i in range(group)])

    for finish in sent:
        finish()
    weight_copy(w, 0, dev_x).wait_send()
    weight_copy(w, 1, dev_p).wait_send()
    weight_copy(w_d, 2, dev_p).wait_send()
    for copy in loss_copies:
        copy.wait_send()


def fused(dims, images, img_pair, texts, txt_pair, gain, perm, right_blocks, left_blocks):
    nb, nn, nw = dims
    group = nn * nw
    devices = nb * group
    t_rows, width = texts.shape
    r_rows = images.shape[0] // group
    block_count, size = right_blocks.shape[:2]
    vmem = pl.BlockSpec(memory_space=pltpu.VMEM)
    hbm = pl.BlockSpec(memory_space=pltpu.HBM)
    dma = pltpu.SemaphoreType.DMA
    grad, loss = pl.pallas_call(
        functools.partial(fused_kernel, dims),
        out_shape=(
            jax.ShapeDtypeStruct((r_rows, width), BF16),
            jax.ShapeDtypeStruct((1, images.shape[0]), F32),
        ),
        in_specs=[hbm] * 8,
        out_specs=(vmem, vmem),
        scratch_shapes=[
            pltpu.VMEM((1, images.shape[0]), jnp.int32),
            pltpu.VMEM((1, t_rows), jnp.int32),
            pltpu.VMEM((1, width), F32),
            pltpu.VMEM((1, width), jnp.int32),
            pltpu.VMEM(right_blocks.shape, BF16),
            pltpu.VMEM(left_blocks.shape, BF16),
            pltpu.VMEM((r_rows, width), BF16),
            pltpu.VMEM((nw, block_count, size, 2 * size), BF16),
            pltpu.VMEM((devices, t_rows, width), BF16),
            pltpu.VMEM((devices, 1, nw * t_rows), jnp.int32),
            pltpu.VMEM((r_rows, width), BF16),
            pltpu.VMEM((r_rows, width), BF16),
            pltpu.VMEM((r_rows, width), BF16),
            pltpu.VMEM((r_rows, width), BF16),
            pltpu.VMEM((nb, r_rows, group * t_rows), F32),
            pltpu.VMEM((group, 1, images.shape[0]), F32),
            dma((8,)),
            dma((3,)),
            dma((nw,)),
            dma((devices, 5, PARTS)),
            dma((devices, PARTS)),
            dma((devices, 5)),
            dma((devices,)),
            dma((group - 1,)),
            dma((group,)),
        ],
        compiler_params=pltpu.CompilerParams(
            collective_id=0, has_side_effects=True, vmem_limit_bytes=67_043_328
        ),
    )(
        images, img_pair[None], texts, txt_pair[None], gain[None], perm[None], right_blocks, left_blocks
    )
    return grad, loss[0]


def monarch(images, gain, perm, right_full, left_full):
    row_count, width = images.shape
    block_count, block_size = (right_full.shape[0], right_full.shape[1])
    values = images.astype(jnp.float32)
    row_mean = jnp.mean(values, axis=1, keepdims=True)
    centered = values - row_mean
    row_var = jnp.mean(centered * centered, axis=1, keepdims=True)
    normed = (centered * lax.rsqrt(row_var + 1e-05) * gain).astype(jnp.bfloat16)
    inner_mixed = jnp.einsum(
        "rke,kec->rkc",
        normed.reshape(row_count, block_count, block_size),
        right_full,
        preferred_element_type=jnp.float32,
    )
    active = (
        jax.nn.gelu(inner_mixed, approximate=True).astype(jnp.bfloat16).reshape(row_count, width)
    )
    permuted = jnp.take(active, perm, axis=1)
    outer_mixed = jnp.einsum(
        "rke,kec->rkc",
        permuted.reshape(row_count, block_count, block_size),
        left_full,
        preferred_element_type=jnp.float32,
    )
    return (values + outer_mixed.reshape(row_count, width)).astype(jnp.bfloat16)


def per_device(images, img_pair, texts, txt_pair, gain, perm, right_blocks, left_blocks):
    right_full, left_full = (
        lax.all_gather(right_blocks, "weight", axis=0, tiled=True),
        lax.all_gather(left_blocks, "weight", axis=0, tiled=True),
    )
    embedded = monarch(images, gain, perm, right_full, left_full)
    gathered, gathered_pair = (
        lax.all_gather(texts, "batch", axis=0, tiled=True),
        lax.all_gather(txt_pair, "batch", axis=0, tiled=True),
    )
    logit_scale = LOGIT_GAIN / math.sqrt(images.shape[1])
    scores = (
        jnp.einsum("rd,cd->rc", embedded, gathered, preferred_element_type=jnp.float32)
        * logit_scale
    )
    matches = (img_pair[:, None] == gathered_pair[None, :]).astype(jnp.float32)
    local_max = jnp.max(scores, axis=1)
    local_pos = jnp.sum(matches * scores, axis=1)
    row_max = lax.pmax(local_max, ("neg", "weight"))
    shifted = jnp.exp(scores - row_max[:, None])
    totals, positive = lax.psum((jnp.sum(shifted, axis=1), local_pos), ("neg", "weight"))
    row_loss = row_max + jnp.log(totals) - positive
    dscore = (shifted / totals[:, None] - matches).astype(jnp.bfloat16)
    grad_sum = lax.psum_scatter(
        jnp.dot(dscore, gathered, preferred_element_type=jnp.float32),
        ("neg", "weight"),
        scatter_dimension=0,
        tiled=True,
    )
    grad_img = grad_sum.astype(jnp.bfloat16)
    return (grad_img, row_loss)


def solution(mesh):
    dims = tuple(mesh.shape[axis] for axis in ("batch", "neg", "weight"))

    def body(images, img_pair, texts, txt_pair, gain, perm, right_blocks, left_blocks):
        args = (images, img_pair, texts, txt_pair, gain, perm, right_blocks, left_blocks)
        text_bytes = math.prod(dims) * texts.size * texts.dtype.itemsize
        if dims[1:] == (2, 4) and dims[0] >= 3 and texts.shape[0] % (16 * PARTS) == 0 and text_bytes <= VMEM_FOR_TEXTS:
            return fused(dims, *args)
        return per_device(*args)

    return jax.shard_map(
        body,
        mesh=mesh,
        in_specs=(
            P("batch", None),
            P("batch"),
            P(("batch", "neg", "weight"), None),
            P(("batch", "neg", "weight")),
            P(),
            P(),
            P("weight", None, None),
            P("weight", None, None),
        ),
        out_specs=(P(("batch", "neg", "weight"), None), P("batch")),
        check_vma=False,
    )
```
